32 devices in a mesh: pole: 4 (over y, x), row: 2 (over core), col: 4 (over z).
Axes of the slice: x: 2, y: 2, z: 4, core: 2. Of those that a mesh axis runs over, the one named last changes fastest.
Arguments:
- ancestor_inverse: bfloat16 [8, 2, 8192, 8192], P('pole', None, 'row', 'col'), may hold values from -0.0625 to 0.0625
- lower_factor: bfloat16 [2, 2, 256, 8192], P(None, None, 'row', 'col'), may hold values from -6 to 6
- upper_factor: bfloat16 [2, 2, 256, 8192], P(None, None, 'col', 'row'), may hold values from -0.0625 to 0.0625
- diag_inverse: float32 [8, 2, 2, 256, 256], P('pole', None, None, 'row', 'col'), may hold values from -6 to 6
- pole_weights: float32 [8, 2], P('pole'), may hold values from -2 to 2
Outputs:
- column_density: float32 [8192, 2, 256], P('row', None, 'col')
- diag_density: float32 [2, 256, 256], P(None, 'row', 'col')
The draws below stay inside these ranges and needn't reach their ends.
All inputs are finite; a program needn't handle non-finite values.
Results may differ from the reference program's by a relative error of at most 0.0003.
Values may be sent and summed in bfloat16 or wider, within the bound.
No kernel may reach another device: no remote copies, remote signals or barrier semaphores. Data moves between devices by JAX's collectives and lax.ppermute only.
A program may use at most 256 MiB of HBM per device.

```python
import jax
import jax.numpy as jnp
from jax import lax

A = 8192
S = 256
NODES = 2
POLES = 8


def levels(rng, dims, shards, least, largest):
    factor_of = 1.0
    for dim, blocks in shards:
        heights = jax.random.uniform(jax.random.fold_in(jax.random.fold_in(rng, 6), dim), (blocks,), jnp.float32, least / len(shards), largest / len(shards))
        factor_of = factor_of * jnp.repeat(jnp.exp(heights), dims[dim] // blocks).reshape((-1,) + (1,) * (len(dims) - 1 - dim))
    return factor_of


def bell_draw(stream_key, dims, spread, limit, pieces=(), dtype=jnp.bfloat16):
    array = jax.random.normal(stream_key, dims, jnp.float32) * spread
    if len(pieces) > 0:
        array = levels(stream_key, dims, pieces, -0.22, 0.18) * array
    return jnp.clip(array, min=-limit, max=limit).astype(dtype)


def setup_inputs(seed: int = 0) -> dict:
    keys = jax.random.split(jax.random.key(seed), 6)
    ancestor_inverse = bell_draw(keys[0], (POLES, 2, A, A), A ** -0.5, 0.0625, ((0, 4), (2, 2), (3, 4)))
    lower_factor = bell_draw(keys[1], (NODES, 2, S, A), 1.0, 6.0, ((2, 2), (3, 4)))
    upper_factor = bell_draw(keys[2], (NODES, 2, S, A), A ** -0.5, 0.0625, ((2, 4), (3, 2)))
    diag_inverse = bell_draw(keys[3], (POLES, NODES, 2, S, S), 1.0, 6.0, ((0, 4), (3, 2), (4, 4)), jnp.float32)
    pole_weights = bell_draw(keys[4], (POLES, 2), 0.35, 2.0, ((0, 4),), jnp.float32)
    return dict(ancestor_inverse=ancestor_inverse, lower_factor=lower_factor, upper_factor=upper_factor, diag_inverse=diag_inverse, pole_weights=pole_weights)


def reference(ancestor_inverse, lower_factor, upper_factor, diag_inverse, pole_weights):
    flat_lower = lower_factor.reshape(NODES * 2 * S, A)

    def one_pole(carry, inputs):
        block, weights, diagonal = inputs
        z_real, z_imag, w_diag = carry
        from_real = jnp.dot(block[0], flat_lower.T, preferred_element_type=jnp.float32).reshape(A, NODES, 2, S)
        from_imag = jnp.dot(block[1], flat_lower.T, preferred_element_type=jnp.float32).reshape(A, NODES, 2, S)
        column_real = from_imag[:, :, 1] - from_real[:, :, 0]
        column_imag = -(from_real[:, :, 1] + from_imag[:, :, 0])
        z_real = z_real + weights[0] * column_real - weights[1] * column_imag
        z_imag = z_imag + weights[0] * column_imag + weights[1] * column_real
        w_diag = w_diag + weights[0] * diagonal[:, 1] + weights[1] * diagonal[:, 0]
        return (z_real, z_imag, w_diag), None

    start = (jnp.zeros((A, NODES, S), jnp.float32), jnp.zeros((A, NODES, S), jnp.float32),
             jnp.zeros((NODES, S, S), jnp.float32))
    (z_real, z_imag, w_diag), _ = lax.scan(one_pole, start, (ancestor_inverse, pole_weights, diag_inverse))
    upper = upper_factor.astype(jnp.float32)
    imag_part = jnp.einsum("nsi,int->nst", upper[:, 0], z_imag, precision=lax.Precision.HIGHEST)
    imag_part = imag_part + jnp.einsum("nsi,int->nst", upper[:, 1], z_real, precision=lax.Precision.HIGHEST)
    return z_imag, w_diag - imag_part
```

```python
import functools

import jax
import jax.numpy as jnp
from jax import lax
from jax.experimental import pallas as pl
from jax.experimental.pallas import tpu as pltpu
from jax.sharding import PartitionSpec as P


F32 = jnp.float32
BF16 = jnp.bfloat16
LO = jnp.float8_e4m3fn
LO_FACTOR = jnp.float8_e5m2
SPAN = 250.0
PAD = 16
NT = (((1,), (1,)), ((), ()))


def dot_nt(a, b):
    return lax.dot_general(a, b, NT, preferred_element_type=F32)


def encode(x):
    top = jnp.max(jnp.abs(x), axis=0, keepdims=True)
    scale = (top * 1.01).astype(BF16).astype(F32)
    inverse = jnp.where(scale > 1e-30, SPAN / jnp.maximum(scale, 1e-30), 0.0)
    size = jnp.exp2(jnp.abs(x) * inverse - SPAN / 2)
    code = jnp.where(x < 0, -size, size).astype(BF16)
    return code, jnp.broadcast_to(scale, (PAD, x.shape[1])).astype(BF16)


def decode(payload):
    rows = payload.shape[0] - PAD
    code = payload[:rows].astype(F32)
    scale = payload[rows:].astype(F32)[:1] * (1.0 / SPAN)
    size = (jnp.log2(jnp.abs(code)) + SPAN / 2) * scale
    return jnp.where(code < 0, -size, size)


def write_payload(ref, x):
    rows = x.shape[0]
    code, scale = encode(x)
    ref[:rows] = code
    ref[rows:] = scale


def main_body(outs, steps, halves, nodes, base_ref, w_ref, g_ref, *rest):
    s_ref, s8_ref = rest[:2]
    zr_ref, out_refs = rest[-1 - len(outs)], rest[len(rest) - len(outs) :]
    poles = g_ref.shape[0]
    w_real = w_imag = None
    for p in range(poles):
        a, b = w_ref[2 * p], w_ref[2 * p + 1]
        real, imag = g_ref[p, 0].astype(F32), g_ref[p, 1].astype(F32)
        x, y = a * real - b * imag, a * imag + b * real
        w_real = x if w_real is None else w_real + x
        w_imag = y if w_imag is None else w_imag + y
    hi_real, hi_imag = w_real.astype(BF16), w_imag.astype(BF16)
    lo_real = (w_real - hi_real.astype(F32)).astype(LO)
    lo_imag = (w_imag - hi_imag.astype(F32)).astype(LO)
    back = -w_ref[2 * poles]
    x = dot_nt(s_ref[...], hi_real) + dot_nt(s8_ref[...], lo_real)
    y = dot_nt(s_ref[...], hi_imag) + dot_nt(s8_ref[...], lo_imag)
    half = x.shape[0] // (halves * nodes * 2)
    shape = (halves * nodes, 2, half, x.shape[1])
    x, y = x.reshape(shape), y.reshape(shape)
    flat = (halves * nodes * half, x.shape[3])
    zr_ref[...] = ((x[:, 0] - y[:, 1]) * back).reshape(flat)
    z_imag = ((x[:, 1] + y[:, 0]) * back).reshape(flat)
    if any(outs):
        code, scale = encode(z_imag)
    first = 0
    for remote, count, out_ref in zip(outs, steps, out_refs, strict=True):
        j = pl.program_id(0)

        @pl.when((j >= first) & (j < first + count))
        def _(remote=remote, out_ref=out_ref):
            if remote:
                out_ref[: z_imag.shape[0]] = code
                out_ref[z_imag.shape[0] :] = scale
            else:
                out_ref[...] = z_imag

        first += count


def main_call(outs, widths, halves, nodes, tile, scalars, at, weights, blocks, s, s8, real):
    poles, _, rows, cols = blocks.shape
    flat = s.shape[0] // 2
    steps = [w // tile for w in widths]
    aliased = [] if real is None else [real]
    out_specs, out_shape, first = [], [], 0
    for remote, width, count in zip(outs, widths, steps, strict=True):
        height = flat + PAD if remote else flat
        out_specs.append(
            pl.BlockSpec(
                (height, tile),
                lambda j, b, f=first, n=count: (0, jnp.clip(j - f, 0, n - 1)),
            )
        )
        out_shape.append(jax.ShapeDtypeStruct((height, width), BF16 if remote else F32))
        first += count
    whole = pl.BlockSpec(memory_space=pltpu.VMEM)
    grid_spec = pltpu.PrefetchScalarGridSpec(
        num_scalar_prefetch=1,
        grid=(sum(steps),),
        in_specs=[
            pl.BlockSpec(memory_space=pltpu.SMEM),
            pl.BlockSpec((poles, 2, tile, cols), lambda j, b: (0, 0, b[at + j], 0)),
        ]
        + [whole] * 2
        + [pl.BlockSpec(memory_space=pl.ANY)] * len(aliased),
        out_specs=[pl.BlockSpec((flat, tile), lambda j, b: (0, b[at + j]))] + out_specs,
    )
    return pl.pallas_call(
        functools.partial(main_body, outs, steps, halves, nodes),
        grid_spec=grid_spec,
        out_shape=[jax.ShapeDtypeStruct((flat, rows), F32)] + out_shape,
        input_output_aliases={5: 0} if aliased else {},
        compiler_params=pltpu.CompilerParams(vmem_limit_bytes=44 << 20),
        name="products",
    )(scalars, weights, blocks, s, s8, *aliased)


def pole_body(nodes, per_col, n_in, at, where_ref, own_ref, *rest):
    ins, outs, z_ref = rest[:n_in], rest[n_in:-1], rest[-1]
    z = own_ref[...]
    for ref in ins:
        z = z + decode(ref[...])
    z_ref[...] = z.reshape(z_ref.shape)
    for k, out in enumerate(outs):
        h = where_ref[at + 2 * k]
        first = pl.multiple_of(where_ref[at + 2 * k + 1], per_col)
        part = z_ref[h, :, pl.ds(first, per_col), :]
        part = part.reshape(nodes * per_col, part.shape[2])
        if k:
            write_payload(out, part)
        else:
            out[...] = part


def pole_call(halves, nodes, per_col, n_col, tile, scalars, at, own, received):
    flat, width = own.shape
    block = lambda rows: pl.BlockSpec((rows, tile), lambda j, w: (0, j))
    part = nodes * per_col
    return pl.pallas_call(
        functools.partial(pole_body, nodes, per_col, len(received), at),
        grid_spec=pltpu.PrefetchScalarGridSpec(
            num_scalar_prefetch=1,
            grid=(width // tile,),
            in_specs=[block(flat)] + [block(flat + PAD)] * len(received),
            out_specs=[block(part)] + [block(part + PAD)] * (n_col - 1),
            scratch_shapes=[pltpu.VMEM((halves, nodes, flat // (halves * nodes), tile), F32)],
        ),
        out_shape=[jax.ShapeDtypeStruct((part, width), F32)]
        + [jax.ShapeDtypeStruct((part + PAD, width), BF16)] * (n_col - 1),
        name="pole_sum",
    )(scalars, own, *received)


def col_body(n_in, own_ref, *rest):
    ins, (z_ref, out_ref) = rest[:n_in], rest[n_in:]
    z = own_ref[...]
    for ref in ins:
        z = z + decode(ref[...])
    z_ref[...] = z
    write_payload(out_ref, z)


def col_call(tile, own, received):
    part, width = own.shape
    block = lambda rows: pl.BlockSpec((rows, tile), lambda j: (0, j))
    return pl.pallas_call(
        functools.partial(col_body, len(received)),
        grid=(width // tile,),
        in_specs=[block(part)] + [block(part + PAD)] * len(received),
        out_specs=[block(part), block(part + PAD)],
        out_shape=[
            jax.ShapeDtypeStruct((part, width), F32),
            jax.ShapeDtypeStruct((part + PAD, width), BF16),
        ],
        name="col_sum",
    )(own, *received)


def place_body(n_in, at, at_ref, *rest):
    ins, out_ref, z_ref, sems = rest[:n_in], rest[-3], rest[-2], rest[-1]
    width = z_ref.shape[2]
    copies = []
    for k, ref in enumerate(ins):
        z_ref[k] = decode(ref[...])
        first = pl.multiple_of(at_ref[at + k] * 128, 128)
        copy = pltpu.make_async_copy(z_ref.at[k], out_ref.at[:, pl.ds(first, width)], sems.at[k])
        copy.start()
        copies.append(copy)
    for copy in copies:
        copy.wait()


def place_call(rows, scalars, at, payloads, out):
    part, width = payloads[0].shape[0] - PAD, payloads[0].shape[1]
    n = len(payloads)
    aliased = [] if out is None else [out]
    return pl.pallas_call(
        functools.partial(place_body, n, at),
        in_specs=[pl.BlockSpec(memory_space=pltpu.SMEM)]
        + [pl.BlockSpec(memory_space=pltpu.VMEM)] * n
        + [pl.BlockSpec(memory_space=pl.ANY)] * len(aliased),
        out_specs=pl.BlockSpec(memory_space=pl.ANY),
        out_shape=jax.ShapeDtypeStruct((part, rows), F32),
        scratch_shapes=[pltpu.VMEM((n, part, width), F32), pltpu.SemaphoreType.DMA((n,))],
        input_output_aliases={1 + n: 0} if aliased else {},
        compiler_params=pltpu.CompilerParams(vmem_limit_bytes=16 << 20),
        name="place",
    )(scalars, *payloads, *aliased)


def split(x):
    hi = x.astype(BF16)
    return hi, (x - hi.astype(F32)).astype(BF16)


def project_body(halves, nodes, per_col, n_col, direct, pieces, at, where_ref, z_ref, u_ref, *rest):
    piece_refs, outs, acc_ref = rest[:pieces], rest[pieces : pieces + n_col], rest[-1]
    half = z_ref.shape[0] // (halves * nodes)
    step = pl.program_id(0)

    @pl.when(step == 0)
    def _():
        acc_ref[...] = jnp.zeros_like(acc_ref)

    def add(ref):
        for n in range(nodes):
            rows = [split(z_ref[pl.ds((h * nodes + n) * half, half)]) for h in range(halves)]
            both = jnp.concatenate([x[0] for x in rows] + [x[1] for x in rows], axis=0)
            result = dot_nt(both, ref[n])
            for h in range(halves):
                low = result[(halves + h) * half : (halves + h + 1) * half]
                acc_ref[h, n] += result[h * half : (h + 1) * half] + low

    if pieces:
        pl.when(step < direct)(lambda: add(u_ref))
    else:
        add(u_ref)
    for k, ref in enumerate(piece_refs):
        pl.when(step == direct + k)(functools.partial(add, ref))

    @pl.when(step == pl.num_programs(0) - 1)
    def _():
        for k, out in enumerate(outs):
            if at is None:
                out[...] = acc_ref[0]
                continue
            first = pl.multiple_of(where_ref[at + 2 * k + 1], per_col)
            out[...] = acc_ref[where_ref[at + 2 * k], :, pl.ds(first, per_col), :]


def project_call(halves, nodes, per_col, n_col, tile, scalars, at, order, z, u, u_first, direct, pieces=()):
    flat, rows = z.shape
    size = u.shape[1]
    out = jax.ShapeDtypeStruct((nodes, per_col, size), F32)
    rows_of = (lambda j, w: (0, j)) if order is None else (lambda j, w: (0, w[order + j]))
    return pl.pallas_call(
        functools.partial(project_body, halves, nodes, per_col, n_col, direct, len(pieces), at),
        grid_spec=pltpu.PrefetchScalarGridSpec(
            num_scalar_prefetch=1,
            grid=(rows // tile,),
            in_specs=[
                pl.BlockSpec((flat, tile), rows_of),
                pl.BlockSpec(
                    (nodes, size, tile),
                    lambda j, w: (0, 0, u_first + jnp.minimum(j, direct - 1)),
                ),
            ]
            + [pl.BlockSpec((nodes, size, tile), lambda j, w: (0, 0, 0))] * len(pieces),
            out_specs=[pl.BlockSpec(out.shape, lambda j, w: (0, 0, 0))] * n_col,
            scratch_shapes=[pltpu.VMEM((halves, nodes, flat // (halves * nodes), size), F32)],
        ),
        out_shape=[out] * n_col,
        name="project",
    )(scalars, z, u, *pieces)


def peer(i, k, n):
    return i ^ k if n & (n - 1) == 0 else (i + k) % n


def back_peer(i, k, n):
    return i ^ k if n & (n - 1) == 0 else (i + n - k) % n


def send(x, axis, k, n):
    return lax.ppermute(x, axis, [(i, peer(i, k, n)) for i in range(n)])


def tree_sum(parts):
    while len(parts) > 1:
        parts = [a + b for a, b in zip(parts[::2], parts[1::2], strict=True)]
    return parts[0]


def plan_of(rows, n_pole):
    quarter = rows // n_pole
    if quarter % 1024 == 0 and n_pole == 4:
        widths = [quarter * 3 // 4, quarter // 4]
        calls = [[(0, 3)], [(0, 2), (0, 1)], [(1, 3), (0, 0)], [(1, 2), (1, 1)], [(1, 0)]]
        return widths, calls
    return [quarter], [[(0, k)] for k in reversed(range(n_pole))]


def per_device(sizes, ancestor_inverse, lower_factor, upper_factor, diag_inverse, pole_weights):
    n_pole, n_row, n_col = sizes
    poles, _, rows, cols = ancestor_inverse.shape
    nodes, _, s_row, _ = lower_factor.shape
    size = s_row * n_row
    per_col = size // n_col
    p, r, c = (lax.axis_index(name) for name in ("pole", "row", "col"))

    if n_row == 2:
        halves = 2
        other = lax.ppermute(lower_factor, "row", [(0, 1), (1, 0)])
        s = jnp.stack([lower_factor, other]).reshape(nodes * 2 * size, cols)
    else:
        halves = 1
        s = lax.all_gather(lower_factor, "row", axis=2, tiled=True).reshape(-1, cols)
    s8 = s.astype(LO_FACTOR)
    half = size // halves

    top = jnp.max(jnp.abs(pole_weights)) * poles
    scale = jnp.where(top > 0, 2.0**19 / jnp.maximum(top, 1e-30), 1.0)
    weights = jnp.concatenate([(pole_weights * scale).reshape(-1), (1.0 / scale).reshape(1)])

    quarter = rows // n_pole
    widths, calls = plan_of(rows, n_pole)
    firsts = [sum(widths[:g]) for g in range(len(widths))]
    tile = min(256, *widths)
    part = rows // 2 // n_pole if rows // 2 // n_pole % 512 == 0 else 0
    direct = rows - part * n_pole
    step = min(512, direct)

    numbers, starts = [], []
    for runs in calls:
        starts.append(len(numbers))
        for g, k in runs:
            base = (peer(p, k, n_pole) * quarter + firsts[g]) // tile
            numbers += [base + j for j in range(widths[g] // tile)]
    puts = []
    for first in firsts:
        puts.append(len(numbers))
        numbers += [(back_peer(p, k, n_pole) * quarter + first) // 128 for k in range(n_pole)]
    where = len(numbers)
    for k in range(n_col):
        target = peer(c, k, n_col)
        per_half = half // per_col
        h = target // per_half
        numbers += [h ^ r if halves == 2 else h, target % per_half * per_col]
    order = len(numbers)
    numbers += list(range(direct // step))
    if part:
        numbers += [direct // part + back_peer(p, k, n_pole) for k in range(n_pole)]
    scalars = jnp.stack([jnp.asarray(x, jnp.int32) for x in numbers])

    pieces = []
    if part:
        piece = lax.dynamic_slice_in_dim(upper_factor[:, 1], direct + p * part, part, 2)
        piece = lax.all_gather(piece, "col", axis=1, tiled=True)
        pieces = [piece]
        for k in range(1, n_pole):
            pieces.append(send(piece, "pole", k, n_pole))
    upper_real = lax.dynamic_slice_in_dim(upper_factor[:, 0], p * quarter, quarter, 2)
    upper_real = lax.all_gather(upper_real, "col", axis=1, tiled=True)
    upper_imag = upper_factor[:, 1, :, :direct]
    upper_imag = lax.all_gather(upper_imag, "col", axis=1, tiled=True)

    real = out = None
    shared = []
    done = {g: {} for g in range(len(widths))}
    for i, runs in enumerate(calls):
        real, *results = main_call(
            [k > 0 for _, k in runs], [widths[g] for g, _ in runs], halves, nodes, tile,
            scalars, starts[i], weights, ancestor_inverse, s, s8, real,
        )
        for (g, k), result in zip(runs, results, strict=True):
            if k:
                result = send(result, "pole", k, n_pole)
            done[g][k] = result
        for g, got in done.items():
            if got is None or len(got) < n_pole:
                continue
            done[g] = None
            own, received = got[0], [got[k] for k in range(1, n_pole)]
            own, *parts = pole_call(
                halves, nodes, per_col, n_col, tile, scalars, where, own, received
            )
            received = []
            for k, x in enumerate(parts):
                received.append(send(x, "col", k + 1, n_col))
            total, payload = col_call(tile, own, received)
            payloads = [payload]
            for k in range(1, n_pole):
                payloads.append(send(payload, "pole", k, n_pole))
            out = place_call(rows, scalars, puts[g], payloads, out)
            shared += project_call(
                1, nodes, per_col, 1, tile, scalars, None, None, total, upper_real,
                firsts[g] // tile, widths[g] // tile,
            )

    parts = project_call(
        halves, nodes, per_col, n_col, step, scalars, where, order, real, upper_imag, 0,
        direct // step, pieces,
    )
    shared.append(parts[0])
    for k in range(1, n_col):
        shared.append(send(parts[k], "col", k, n_col))
    shared = sum(shared[1:], shared[0])
    weight_real = pole_weights[:, 0].reshape(-1, 1, 1, 1)
    weight_imag = pole_weights[:, 1].reshape(-1, 1, 1, 1)
    weighted_diag = jnp.sum(
        weight_real * diag_inverse[:, :, 1] + weight_imag * diag_inverse[:, :, 0], axis=0
    ).transpose(0, 2, 1)
    if n_row == 2:
        keep = lax.dynamic_slice_in_dim(shared, r * s_row, s_row, 2)
        give = lax.dynamic_slice_in_dim(shared, (1 - r) * s_row, s_row, 2)
        shared = keep + lax.ppermute(give, "row", [(0, 1), (1, 0)])
    else:
        shared = lax.psum_scatter(shared, "row", scatter_dimension=2, tiled=True)
    mine = weighted_diag - shared
    if n_pole & (n_pole - 1) == 0:
        terms = [mine]
        for k in range(1, n_pole):
            terms.append(send(mine, "pole", k, n_pole))
        diag = tree_sum(terms)
    else:
        diag = lax.psum(mine, "pole")
    density = out.reshape(nodes, per_col, rows).transpose(2, 0, 1)
    return density, diag.transpose(0, 2, 1)


def solution(mesh):
    sizes = tuple(mesh.shape[name] for name in ("pole", "row", "col"))
    placed = (
        P("pole", None, "row", "col"),
        P(None, None, "row", "col"),
        P(None, None, "col", "row"),
        P("pole", None, None, "row", "col"),
        P("pole", None),
    )

    def body(ancestor_inverse, *rest):
        return per_device(sizes, ancestor_inverse, *rest)

    return jax.shard_map(
        body,
        mesh=mesh,
        in_specs=placed,
        out_specs=(P("row", None, "col"), P(None, "row", "col")),
        check_vma=False,
    )
```

```python
import functools

import jax
import jax.numpy as jnp
from jax import lax
from jax.experimental import pallas as pl
from jax.experimental.pallas import tpu as pltpu
from jax.sharding import PartitionSpec as P


F32 = jnp.float32
BF16 = jnp.bfloat16
LO = jnp.float8_e4m3fn
LO_FACTOR = jnp.float8_e5m2
SPAN = 250.0
PAD = 16
NT = (((1,), (1,)), ((), ()))


def dot_nt(a, b):
    return lax.dot_general(a, b, NT, preferred_element_type=F32)


def encode(x):
    top = jnp.max(jnp.abs(x), axis=0, keepdims=True)
    scale = (top * 1.01).astype(BF16).astype(F32)
    inverse = jnp.where(scale > 1e-30, SPAN / jnp.maximum(scale, 1e-30), 0.0)
    size = jnp.exp2(jnp.abs(x) * inverse - SPAN / 2)
    code = jnp.where(x < 0, -size, size).astype(BF16)
    return code, jnp.broadcast_to(scale, (PAD, x.shape[1])).astype(BF16)


def decode(payload):
    rows = payload.shape[0] - PAD
    code = payload[:rows].astype(F32)
    scale = payload[rows:].astype(F32)[:1] * (1.0 / SPAN)
    size = (jnp.log2(jnp.abs(code)) + SPAN / 2) * scale
    return jnp.where(code < 0, -size, size)


def write_payload(ref, x):
    rows = x.shape[0]
    code, scale = encode(x)
    ref[:rows] = code
    ref[rows:] = scale


def main_body(outs, steps, halves, nodes, base_ref, w_ref, g_ref, *rest):
    s_ref, s8_ref = rest[:2]
    zr_ref, out_refs = rest[-1 - len(outs)], rest[len(rest) - len(outs) :]
    poles = g_ref.shape[0]
    w_real = w_imag = None
    for p in range(poles):
        a, b = w_ref[2 * p], w_ref[2 * p + 1]
        real, imag = g_ref[p, 0].astype(F32), g_ref[p, 1].astype(F32)
        x, y = a * real - b * imag, a * imag + b * real
        w_real = x if w_real is None else w_real + x
        w_imag = y if w_imag is None else w_imag + y
    hi_real, hi_imag = w_real.astype(BF16), w_imag.astype(BF16)
    lo_real = (w_real - hi_real.astype(F32)).astype(LO)
    lo_imag = (w_imag - hi_imag.astype(F32)).astype(LO)
    back = -w_ref[2 * poles]
    x = dot_nt(s_ref[...], hi_real) + dot_nt(s8_ref[...], lo_real)
    y = dot_nt(s_ref[...], hi_imag) + dot_nt(s8_ref[...], lo_imag)
    half = x.shape[0] // (halves * nodes * 2)
    shape = (halves * nodes, 2, half, x.shape[1])
    x, y = x.reshape(shape), y.reshape(shape)
    flat = (halves * nodes * half, x.shape[3])
    zr_ref[...] = ((x[:, 0] - y[:, 1]) * back).reshape(flat)
    z_imag = ((x[:, 1] + y[:, 0]) * back).reshape(flat)
    if any(outs):
        code, scale = encode(z_imag)
    first = 0
    for remote, count, out_ref in zip(outs, steps, out_refs, strict=True):
        j = pl.program_id(0)

        @pl.when((j >= first) & (j < first + count))
        def _(remote=remote, out_ref=out_ref):
            if remote:
                out_ref[: z_imag.shape[0]] = code
                out_ref[z_imag.shape[0] :] = scale
            else:
                out_ref[...] = z_imag

        first += count


def main_call(outs, widths, halves, nodes, tile, scalars, at, weights, blocks, s, s8, real):
    poles, _, rows, cols = blocks.shape
    flat = s.shape[0] // 2
    steps = [w // tile for w in widths]
    aliased = [] if real is None else [real]
    out_specs, out_shape, first = [], [], 0
    for remote, width, count in zip(outs, widths, steps, strict=True):
        height = flat + PAD if remote else flat
        out_specs.append(
            pl.BlockSpec(
                (height, tile),
                lambda j, b, f=first, n=count: (0, jnp.clip(j - f, 0, n - 1)),
            )
        )
        out_shape.append(jax.ShapeDtypeStruct((height, width), BF16 if remote else F32))
        first += count
    whole = pl.BlockSpec(memory_space=pltpu.VMEM)
    grid_spec = pltpu.PrefetchScalarGridSpec(
        num_scalar_prefetch=1,
        grid=(sum(steps),),
        in_specs=[
            pl.BlockSpec(memory_space=pltpu.SMEM),
            pl.BlockSpec((poles, 2, tile, cols), lambda j, b: (0, 0, b[at + j], 0)),
        ]
        + [whole] * 2
        + [pl.BlockSpec(memory_space=pl.ANY)] * len(aliased),
        out_specs=[pl.BlockSpec((flat, tile), lambda j, b: (0, b[at + j]))] + out_specs,
    )
    return pl.pallas_call(
        functools.partial(main_body, outs, steps, halves, nodes),
        grid_spec=grid_spec,
        out_shape=[jax.ShapeDtypeStruct((flat, rows), F32)] + out_shape,
        input_output_aliases={5: 0} if aliased else {},
        compiler_params=pltpu.CompilerParams(vmem_limit_bytes=32 << 20),
        name="products",
    )(scalars, weights, blocks, s, s8, *aliased)


def pole_body(nodes, per_col, n_in, at, where_ref, own_ref, *rest):
    ins, outs, z_ref = rest[:n_in], rest[n_in:-1], rest[-1]
    z = own_ref[...]
    for ref in ins:
        z = z + decode(ref[...])
    z_ref[...] = z.reshape(z_ref.shape)
    for k, out in enumerate(outs):
        h = where_ref[at + 2 * k]
        first = pl.multiple_of(where_ref[at + 2 * k + 1], per_col)
        part = z_ref[h, :, pl.ds(first, per_col), :]
        part = part.reshape(nodes * per_col, part.shape[2])
        if k:
            write_payload(out, part)
        else:
            out[...] = part


def pole_call(halves, nodes, per_col, n_col, tile, scalars, at, own, received):
    flat, width = own.shape
    block = lambda rows: pl.BlockSpec((rows, tile), lambda j, w: (0, j))
    part = nodes * per_col
    return pl.pallas_call(
        functools.partial(pole_body, nodes, per_col, len(received), at),
        grid_spec=pltpu.PrefetchScalarGridSpec(
            num_scalar_prefetch=1,
            grid=(width // tile,),
            in_specs=[block(flat)] + [block(flat + PAD)] * len(received),
            out_specs=[block(part)] + [block(part + PAD)] * (n_col - 1),
            scratch_shapes=[pltpu.VMEM((halves, nodes, flat // (halves * nodes), tile), F32)],
        ),
        out_shape=[jax.ShapeDtypeStruct((part, width), F32)]
        + [jax.ShapeDtypeStruct((part + PAD, width), BF16)] * (n_col - 1),
        compiler_params=pltpu.CompilerParams(vmem_limit_bytes=16 << 20),
        name="pole_sum",
    )(scalars, own, *received)


def col_body(n_in, nodes, own_ref, u_ref, *rest):
    ins, (shared_ref, out_ref) = rest[:n_in], rest[n_in:]
    z = own_ref[...]
    for ref in ins:
        z = z + decode(ref[...])
    write_payload(out_ref, z)
    half = z.shape[0] // nodes
    hi, lo = split(z)

    @pl.when(pl.program_id(0) == 0)
    def _():
        shared_ref[...] = jnp.zeros_like(shared_ref)

    for n in range(nodes):
        rows = slice(n * half, (n + 1) * half)
        shared_ref[n] += dot_nt(hi[rows], u_ref[n]) + dot_nt(lo[rows], u_ref[n])


def col_call(tile, nodes, own, received, u, first):
    part, width = own.shape
    size = u.shape[1]
    block = lambda rows: pl.BlockSpec((rows, tile), lambda j: (0, j))
    shared = jax.ShapeDtypeStruct((nodes, part // nodes, size), F32)
    return pl.pallas_call(
        functools.partial(col_body, len(received), nodes),
        grid=(width // tile,),
        in_specs=[
            block(part),
            pl.BlockSpec((nodes, size, tile), lambda j: (0, 0, first // tile + j)),
        ]
        + [block(part + PAD)] * len(received),
        out_specs=[pl.BlockSpec(shared.shape, lambda j: (0, 0, 0)), block(part + PAD)],
        out_shape=[shared, jax.ShapeDtypeStruct((part + PAD, width), BF16)],
        compiler_params=pltpu.CompilerParams(vmem_limit_bytes=16 << 20),
        name="col_sum",
    )(own, u, *received)


def place_body(n_in, at, at_ref, *rest):
    ins, out_ref, z_ref, sems = rest[:n_in], rest[-3], rest[-2], rest[-1]
    width = z_ref.shape[2]
    copies = []
    for k, ref in enumerate(ins):
        z_ref[k] = decode(ref[...])
        first = pl.multiple_of(at_ref[at + k] * 128, 128)
        copy = pltpu.make_async_copy(z_ref.at[k], out_ref.at[:, pl.ds(first, width)], sems.at[k])
        copy.start()
        copies.append(copy)
    for copy in copies:
        copy.wait()


def place_call(rows, scalars, at, payloads, out):
    part, width = payloads[0].shape[0] - PAD, payloads[0].shape[1]
    n = len(payloads)
    aliased = [] if out is None else [out]
    return pl.pallas_call(
        functools.partial(place_body, n, at),
        in_specs=[pl.BlockSpec(memory_space=pltpu.SMEM)]
        + [pl.BlockSpec(memory_space=pltpu.VMEM)] * n
        + [pl.BlockSpec(memory_space=pl.ANY)] * len(aliased),
        out_specs=pl.BlockSpec(memory_space=pl.ANY),
        out_shape=jax.ShapeDtypeStruct((part, rows), F32),
        scratch_shapes=[pltpu.VMEM((n, part, width), F32), pltpu.SemaphoreType.DMA((n,))],
        input_output_aliases={1 + n: 0} if aliased else {},
        compiler_params=pltpu.CompilerParams(vmem_limit_bytes=16 << 20),
        name="place",
    )(scalars, *payloads, *aliased)


def split(x):
    hi = x.astype(BF16)
    return hi, (x - hi.astype(F32)).astype(BF16)


def project_body(halves, nodes, per_col, n_col, at, where_ref, z_ref, u_ref, *rest):
    outs, acc_ref = rest[:n_col], rest[-1]
    half = z_ref.shape[0] // (halves * nodes)
    step = pl.program_id(0)

    @pl.when(step == 0)
    def _():
        acc_ref[...] = jnp.zeros_like(acc_ref)

    for n in range(nodes):
        rows = [split(z_ref[pl.ds((h * nodes + n) * half, half)]) for h in range(halves)]
        both = jnp.concatenate([x[0] for x in rows] + [x[1] for x in rows], axis=0)
        result = dot_nt(both, u_ref[n])
        for h in range(halves):
            low = result[(halves + h) * half : (halves + h + 1) * half]
            acc_ref[h, n] += result[h * half : (h + 1) * half] + low

    @pl.when(step == pl.num_programs(0) - 1)
    def _():
        for k, out in enumerate(outs):
            first = pl.multiple_of(where_ref[at + 2 * k + 1], per_col)
            out[...] = acc_ref[where_ref[at + 2 * k], :, pl.ds(first, per_col), :]


def project_call(halves, nodes, per_col, n_col, tile, scalars, at, z, u):
    flat, rows = z.shape
    size = u.shape[1]
    out = jax.ShapeDtypeStruct((nodes, per_col, size), F32)
    return pl.pallas_call(
        functools.partial(project_body, halves, nodes, per_col, n_col, at),
        grid_spec=pltpu.PrefetchScalarGridSpec(
            num_scalar_prefetch=1,
            grid=(rows // tile,),
            in_specs=[
                pl.BlockSpec((flat, tile), lambda j, w: (0, j)),
                pl.BlockSpec((nodes, size, tile), lambda j, w: (0, 0, j)),
            ],
            out_specs=[pl.BlockSpec(out.shape, lambda j, w: (0, 0, 0))] * n_col,
            scratch_shapes=[pltpu.VMEM((halves, nodes, flat // (halves * nodes), size), F32)],
        ),
        out_shape=[out] * n_col,
        compiler_params=pltpu.CompilerParams(vmem_limit_bytes=24 << 20),
        name="project",
    )(scalars, z, u)


def peer(i, k, n):
    return i ^ k if n & (n - 1) == 0 else (i + k) % n


def back_peer(i, k, n):
    return i ^ k if n & (n - 1) == 0 else (i + n - k) % n


def send(x, axis, k, n):
    return lax.ppermute(x, axis, [(i, peer(i, k, n)) for i in range(n)])


def tree_sum(parts):
    while len(parts) > 1:
        parts = [a + b for a, b in zip(parts[::2], parts[1::2], strict=True)]
    return parts[0]


def plan_of(rows, n_pole):
    quarter = rows // n_pole
    if quarter % 1024 == 0 and n_pole == 4:
        widths = [quarter * 3 // 4, quarter // 4]
        calls = [[(0, 3)], [(0, 2), (0, 1)], [(1, 3), (0, 0)], [(1, 2), (1, 1)], [(1, 0)]]
        return widths, calls
    return [quarter], [[(0, k)] for k in reversed(range(n_pole))]


def per_device(sizes, ancestor_inverse, lower_factor, upper_factor, diag_inverse, pole_weights):
    n_pole, n_row, n_col = sizes
    poles, _, rows, cols = ancestor_inverse.shape
    nodes, _, s_row, _ = lower_factor.shape
    size = s_row * n_row
    per_col = size // n_col
    p, r, c = (lax.axis_index(name) for name in ("pole", "row", "col"))

    if n_row == 2:
        halves = 2
        other = lax.ppermute(lower_factor, "row", [(0, 1), (1, 0)])
        s = jnp.stack([lower_factor, other]).reshape(nodes * 2 * size, cols)
    else:
        halves = 1
        s = lax.all_gather(lower_factor, "row", axis=2, tiled=True).reshape(-1, cols)
    s8 = s.astype(LO_FACTOR)
    half = size // halves

    top = jnp.max(jnp.abs(pole_weights)) * poles
    scale = jnp.where(top > 0, 2.0**19 / jnp.maximum(top, 1e-30), 1.0)
    weights = jnp.concatenate([(pole_weights * scale).reshape(-1), (1.0 / scale).reshape(1)])

    quarter = rows // n_pole
    widths, calls = plan_of(rows, n_pole)
    firsts = [sum(widths[:g]) for g in range(len(widths))]
    tile = min(256, *widths)
    step = min(1024, rows)

    numbers, starts = [], []
    for runs in calls:
        starts.append(len(numbers))
        for g, k in runs:
            base = (peer(p, k, n_pole) * quarter + firsts[g]) // tile
            numbers += [base + j for j in range(widths[g] // tile)]
    puts = []
    for first in firsts:
        puts.append(len(numbers))
        numbers += [(back_peer(p, k, n_pole) * quarter + first) // 128 for k in range(n_pole)]
    where = len(numbers)
    for k in range(n_col):
        target = peer(c, k, n_col)
        per_half = half // per_col
        h = target // per_half
        numbers += [h ^ r if halves == 2 else h, target % per_half * per_col]
    scalars = jnp.stack([jnp.asarray(x, jnp.int32) for x in numbers])

    upper_imag = upper_factor[:, 1]
    upper_imag = lax.all_gather(upper_imag, "col", axis=1, tiled=True)
    upper_real = lax.dynamic_slice_in_dim(upper_factor[:, 0], p * quarter, quarter, 2)
    upper_real = lax.all_gather(upper_real, "col", axis=1, tiled=True)

    real = out = None
    shared = []
    done = {g: {} for g in range(len(widths))}
    for i, runs in enumerate(calls):
        real, *results = main_call(
            [k > 0 for _, k in runs], [widths[g] for g, _ in runs], halves, nodes, tile,
            scalars, starts[i], weights, ancestor_inverse, s, s8, real,
        )
        for (g, k), result in zip(runs, results, strict=True):
            if k:
                result = send(result, "pole", k, n_pole)
            done[g][k] = result
        for g, got in done.items():
            if got is None or len(got) < n_pole:
                continue
            done[g] = None
            own, received = got[0], [got[k] for k in range(1, n_pole)]
            own, *parts = pole_call(
                halves, nodes, per_col, n_col, tile, scalars, where, own, received
            )
            received = []
            for k, x in enumerate(parts):
                received.append(send(x, "col", k + 1, n_col))
            projected, payload = col_call(tile, nodes, own, received, upper_real, firsts[g])
            shared.append(projected)
            payloads = [payload]
            for k in range(1, n_pole):
                payloads.append(send(payload, "pole", k, n_pole))
            out = place_call(rows, scalars, puts[g], payloads, out)

    parts = project_call(
        halves, nodes, per_col, n_col, step, scalars, where, real, upper_imag
    )
    shared.append(parts[0])
    for k in range(1, n_col):
        shared.append(send(parts[k], "col", k, n_col))
    shared = sum(shared[1:], shared[0])
    weight_real = pole_weights[:, 0].reshape(-1, 1, 1, 1)
    weight_imag = pole_weights[:, 1].reshape(-1, 1, 1, 1)
    weighted_diag = jnp.sum(
        weight_real * diag_inverse[:, :, 1] + weight_imag * diag_inverse[:, :, 0], axis=0
    ).transpose(0, 2, 1)
    if n_row == 2:
        keep = lax.dynamic_slice_in_dim(shared, r * s_row, s_row, 2)
        give = lax.dynamic_slice_in_dim(shared, (1 - r) * s_row, s_row, 2)
        shared = keep + lax.ppermute(give, "row", [(0, 1), (1, 0)])
    else:
        shared = lax.psum_scatter(shared, "row", scatter_dimension=2, tiled=True)
    mine = weighted_diag - shared
    if n_pole & (n_pole - 1) == 0:
        terms = [mine]
        for k in range(1, n_pole):
            terms.append(send(mine, "pole", k, n_pole))
        diag = tree_sum(terms)
    else:
        diag = lax.psum(mine, "pole")
    density = out.reshape(nodes, per_col, rows).transpose(2, 0, 1)
    return density, diag.transpose(0, 2, 1)


def solution(mesh):
    sizes = tuple(mesh.shape[name] for name in ("pole", "row", "col"))
    placed = (
        P("pole", None, "row", "col"),
        P(None, None, "row", "col"),
        P(None, None, "col", "row"),
        P("pole", None, None, "row", "col"),
        P("pole", None),
    )

    def body(ancestor_inverse, *rest):
        return per_device(sizes, ancestor_inverse, *rest)

    return jax.shard_map(
        body,
        mesh=mesh,
        in_specs=placed,
        out_specs=(P("row", None, "col"), P(None, "row", "col")),
        check_vma=False,
    )
```

```python
import functools

import jax
import jax.numpy as jnp
from jax import lax
from jax.experimental import pallas as pl
from jax.experimental.pallas import tpu as pltpu
from jax.sharding import PartitionSpec as P


F32 = jnp.float32
BF16 = jnp.bfloat16
LO = jnp.float8_e4m3fn
LO_FACTOR = jnp.float8_e5m2
SPAN = 250.0
PAD = 16
NT = (((1,), (1,)), ((), ()))


def dot_nt(a, b):
    return lax.dot_general(a, b, NT, preferred_element_type=F32)


def encode(x):
    top = jnp.max(jnp.abs(x), axis=0, keepdims=True)
    scale = (top * 1.01).astype(BF16).astype(F32)
    inverse = jnp.where(scale > 1e-30, SPAN / jnp.maximum(scale, 1e-30), 0.0)
    size = jnp.exp2(jnp.abs(x) * inverse - SPAN / 2)
    code = jnp.where(x < 0, -size, size).astype(BF16)
    return code, jnp.broadcast_to(scale, (PAD, x.shape[1])).astype(BF16)


def decode(payload):
    rows = payload.shape[0] - PAD
    code = payload[:rows].astype(F32)
    scale = payload[rows:].astype(F32)[:1] * (1.0 / SPAN)
    size = (jnp.log2(jnp.abs(code)) + SPAN / 2) * scale
    return jnp.where(code < 0, -size, size)


def write_payload(ref, x):
    rows = x.shape[0]
    code, scale = encode(x)
    ref[:rows] = code
    ref[rows:] = scale


def main_body(outs, steps, halves, nodes, base_ref, w_ref, g_ref, *rest):
    s_ref, s8_ref = rest[:2]
    zr_ref, out_refs = rest[-1 - len(outs)], rest[len(rest) - len(outs) :]
    poles = g_ref.shape[0]
    w_real = w_imag = None
    for p in range(poles):
        a, b = w_ref[2 * p], w_ref[2 * p + 1]
        real, imag = g_ref[p, 0].astype(F32), g_ref[p, 1].astype(F32)
        x, y = a * real - b * imag, a * imag + b * real
        w_real = x if w_real is None else w_real + x
        w_imag = y if w_imag is None else w_imag + y
    hi_real, hi_imag = w_real.astype(BF16), w_imag.astype(BF16)
    lo_real = (w_real - hi_real.astype(F32)).astype(LO)
    lo_imag = (w_imag - hi_imag.astype(F32)).astype(LO)
    back = -w_ref[2 * poles]
    x = dot_nt(s_ref[...], hi_real) + dot_nt(s8_ref[...], lo_real)
    y = dot_nt(s_ref[...], hi_imag) + dot_nt(s8_ref[...], lo_imag)
    half = x.shape[0] // (halves * nodes * 2)
    shape = (halves * nodes, 2, half, x.shape[1])
    x, y = x.reshape(shape), y.reshape(shape)
    flat = (halves * nodes * half, x.shape[3])
    zr_ref[...] = ((x[:, 0] - y[:, 1]) * back).reshape(flat)
    z_imag = ((x[:, 1] + y[:, 0]) * back).reshape(flat)
    if any(outs):
        code, scale = encode(z_imag)
    first = 0
    for remote, count, out_ref in zip(outs, steps, out_refs, strict=True):
        j = pl.program_id(0)

        @pl.when((j >= first) & (j < first + count))
        def _(remote=remote, out_ref=out_ref):
            if remote:
                out_ref[: z_imag.shape[0]] = code
                out_ref[z_imag.shape[0] :] = scale
            else:
                out_ref[...] = z_imag

        first += count


def main_call(outs, widths, halves, nodes, tile, scalars, at, weights, blocks, s, s8, real):
    poles, _, rows, cols = blocks.shape
    flat = s.shape[0] // 2
    steps = [w // tile for w in widths]
    aliased = [] if real is None else [real]
    out_specs, out_shape, first = [], [], 0
    for remote, width, count in zip(outs, widths, steps, strict=True):
        height = flat + PAD if remote else flat
        out_specs.append(
            pl.BlockSpec(
                (height, tile),
                lambda j, b, f=first, n=count: (0, jnp.clip(j - f, 0, n - 1)),
            )
        )
        out_shape.append(jax.ShapeDtypeStruct((height, width), BF16 if remote else F32))
        first += count
    whole = pl.BlockSpec(memory_space=pltpu.VMEM)
    grid_spec = pltpu.PrefetchScalarGridSpec(
        num_scalar_prefetch=1,
        grid=(sum(steps),),
        in_specs=[
            pl.BlockSpec(memory_space=pltpu.SMEM),
            pl.BlockSpec((poles, 2, tile, cols), lambda j, b: (0, 0, b[at + j], 0)),
        ]
        + [whole] * 2
        + [pl.BlockSpec(memory_space=pl.ANY)] * len(aliased),
        out_specs=[pl.BlockSpec((flat, tile), lambda j, b: (0, b[at + j]))] + out_specs,
    )
    return pl.pallas_call(
        functools.partial(main_body, outs, steps, halves, nodes),
        grid_spec=grid_spec,
        out_shape=[jax.ShapeDtypeStruct((flat, rows), F32)] + out_shape,
        input_output_aliases={5: 0} if aliased else {},
        compiler_params=pltpu.CompilerParams(vmem_limit_bytes=32 << 20),
        name="products",
    )(scalars, weights, blocks, s, s8, *aliased)


def pole_body(nodes, per_col, n_in, at, where_ref, own_ref, *rest):
    ins, outs, z_ref = rest[:n_in], rest[n_in:-1], rest[-1]
    z = own_ref[...]
    for ref in ins:
        z = z + decode(ref[...])
    z_ref[...] = z.reshape(z_ref.shape)
    for k, out in enumerate(outs):
        h = where_ref[at + 2 * k]
        first = pl.multiple_of(where_ref[at + 2 * k + 1], per_col)
        part = z_ref[h, :, pl.ds(first, per_col), :]
        part = part.reshape(nodes * per_col, part.shape[2])
        if k:
            write_payload(out, part)
        else:
            out[...] = part


def pole_call(halves, nodes, per_col, n_col, tile, scalars, at, own, received):
    flat, width = own.shape
    block = lambda rows: pl.BlockSpec((rows, tile), lambda j, w: (0, j))
    part = nodes * per_col
    return pl.pallas_call(
        functools.partial(pole_body, nodes, per_col, len(received), at),
        grid_spec=pltpu.PrefetchScalarGridSpec(
            num_scalar_prefetch=1,
            grid=(width // tile,),
            in_specs=[block(flat)] + [block(flat + PAD)] * len(received),
            out_specs=[block(part)] + [block(part + PAD)] * (n_col - 1),
            scratch_shapes=[pltpu.VMEM((halves, nodes, flat // (halves * nodes), tile), F32)],
        ),
        out_shape=[jax.ShapeDtypeStruct((part, width), F32)]
        + [jax.ShapeDtypeStruct((part + PAD, width), BF16)] * (n_col - 1),
        compiler_params=pltpu.CompilerParams(vmem_limit_bytes=16 << 20),
        name="pole_sum",
    )(scalars, own, *received)


def gathered(u_refs, all_ref, owner_ref, at):
    for k, ref in enumerate(u_refs):
        all_ref[owner_ref[at + k]] = ref[...]
    blocks, nodes = all_ref.shape[:2]
    return [jnp.concatenate([all_ref[k, n] for k in range(blocks)], axis=0) for n in range(nodes)]


def col_body(nodes, n_col, at, owner_ref, own_ref, *rest):
    u_refs, ins, (shared_ref, out_ref, all_ref) = rest[:n_col], rest[n_col:-3], rest[-3:]
    u = gathered(u_refs, all_ref, owner_ref, at)
    z = own_ref[...]
    for ref in ins:
        z = z + decode(ref[...])
    write_payload(out_ref, z)
    half = z.shape[0] // nodes
    hi, lo = split(z)

    @pl.when(pl.program_id(0) == 0)
    def _():
        shared_ref[...] = jnp.zeros_like(shared_ref)

    for n in range(nodes):
        rows = slice(n * half, (n + 1) * half)
        shared_ref[n] += dot_nt(hi[rows], u[n]) + dot_nt(lo[rows], u[n])


def col_call(tile, nodes, scalars, at, own, received, u, first):
    part, width = own.shape
    block = lambda rows: pl.BlockSpec((rows, tile), lambda j, w: (0, j))
    some = u[0].shape[1]
    shared = jax.ShapeDtypeStruct((nodes, part // nodes, some * len(u)), F32)
    return pl.pallas_call(
        functools.partial(col_body, nodes, len(u), at),
        grid_spec=pltpu.PrefetchScalarGridSpec(
            num_scalar_prefetch=1,
            grid=(width // tile,),
            in_specs=[block(part)]
            + [pl.BlockSpec((nodes, some, tile), lambda j, w: (0, 0, first // tile + j))] * len(u)
            + [block(part + PAD)] * len(received),
            out_specs=[pl.BlockSpec(shared.shape, lambda j, w: (0, 0, 0)), block(part + PAD)],
            scratch_shapes=[pltpu.VMEM((len(u), nodes, some, tile), BF16)],
        ),
        out_shape=[shared, jax.ShapeDtypeStruct((part + PAD, width), BF16)],
        compiler_params=pltpu.CompilerParams(vmem_limit_bytes=16 << 20),
        name="col_sum",
    )(scalars, own, *u, *received)


def place_body(n_in, at, at_ref, *rest):
    ins, out_ref, z_ref, sems = rest[:n_in], rest[-3], rest[-2], rest[-1]
    width = z_ref.shape[2]
    copies = []
    for k, ref in enumerate(ins):
        z_ref[k] = decode(ref[...])
        first = pl.multiple_of(at_ref[at + k] * 128, 128)
        copy = pltpu.make_async_copy(z_ref.at[k], out_ref.at[:, pl.ds(first, width)], sems.at[k])
        copy.start()
        copies.append(copy)
    for copy in copies:
        copy.wait()


def place_call(rows, scalars, at, payloads, out):
    part, width = payloads[0].shape[0] - PAD, payloads[0].shape[1]
    n = len(payloads)
    aliased = [] if out is None else [out]
    return pl.pallas_call(
        functools.partial(place_body, n, at),
        in_specs=[pl.BlockSpec(memory_space=pltpu.SMEM)]
        + [pl.BlockSpec(memory_space=pltpu.VMEM)] * n
        + [pl.BlockSpec(memory_space=pl.ANY)] * len(aliased),
        out_specs=pl.BlockSpec(memory_space=pl.ANY),
        out_shape=jax.ShapeDtypeStruct((part, rows), F32),
        scratch_shapes=[pltpu.VMEM((n, part, width), F32), pltpu.SemaphoreType.DMA((n,))],
        input_output_aliases={1 + n: 0} if aliased else {},
        compiler_params=pltpu.CompilerParams(vmem_limit_bytes=16 << 20),
        name="place",
    )(scalars, *payloads, *aliased)


def split(x):
    hi = x.astype(BF16)
    return hi, (x - hi.astype(F32)).astype(BF16)


def project_body(halves, nodes, per_col, n_col, at, owners, where_ref, z_ref, *rest):
    u_refs, outs, (acc_ref, all_ref) = rest[:n_col], rest[n_col:-2], rest[-2:]
    u = gathered(u_refs, all_ref, where_ref, owners)
    half = z_ref.shape[0] // (halves * nodes)
    step = pl.program_id(0)

    @pl.when(step == 0)
    def _():
        acc_ref[...] = jnp.zeros_like(acc_ref)

    for n in range(nodes):
        rows = [split(z_ref[pl.ds((h * nodes + n) * half, half)]) for h in range(halves)]
        both = jnp.concatenate([x[0] for x in rows] + [x[1] for x in rows], axis=0)
        result = dot_nt(both, u[n])
        for h in range(halves):
            low = result[(halves + h) * half : (halves + h + 1) * half]
            acc_ref[h, n] += result[h * half : (h + 1) * half] + low

    @pl.when(step == pl.num_programs(0) - 1)
    def _():
        for k, out in enumerate(outs):
            first = pl.multiple_of(where_ref[at + 2 * k + 1], per_col)
            out[...] = acc_ref[where_ref[at + 2 * k], :, pl.ds(first, per_col), :]


def project_call(halves, nodes, per_col, n_col, tile, scalars, at, owners, z, u):
    flat, rows = z.shape
    some = u[0].shape[1]
    size = some * n_col
    out = jax.ShapeDtypeStruct((nodes, per_col, size), F32)
    return pl.pallas_call(
        functools.partial(project_body, halves, nodes, per_col, n_col, at, owners),
        grid_spec=pltpu.PrefetchScalarGridSpec(
            num_scalar_prefetch=1,
            grid=(rows // tile,),
            in_specs=[
                pl.BlockSpec((flat, tile), lambda j, w: (0, j)),
            ]
            + [pl.BlockSpec((nodes, some, tile), lambda j, w: (0, 0, j))] * n_col,
            out_specs=[pl.BlockSpec(out.shape, lambda j, w: (0, 0, 0))] * n_col,
            scratch_shapes=[
                pltpu.VMEM((halves, nodes, flat // (halves * nodes), size), F32),
                pltpu.VMEM((n_col, nodes, some, tile), BF16),
            ],
        ),
        out_shape=[out] * n_col,
        compiler_params=pltpu.CompilerParams(vmem_limit_bytes=24 << 20),
        name="project",
    )(scalars, z, *u)


def peer(i, k, n):
    return i ^ k if n & (n - 1) == 0 else (i + k) % n


def back_peer(i, k, n):
    return i ^ k if n & (n - 1) == 0 else (i + n - k) % n


def send(x, axis, k, n):
    return lax.ppermute(x, axis, [(i, peer(i, k, n)) for i in range(n)])


def tree_sum(parts):
    while len(parts) > 1:
        parts = [a + b for a, b in zip(parts[::2], parts[1::2], strict=True)]
    return parts[0]


def plan_of(rows, n_pole):
    quarter = rows // n_pole
    if quarter % 1024 == 0 and n_pole == 4:
        widths = [quarter * 3 // 4, quarter // 4]
        calls = [[(0, 3), (0, 2)], [(0, 1), (0, 0)], [(1, 3), (1, 2), (1, 1)], [(1, 0)]]
        return widths, calls
    return [quarter], [[(0, k)] for k in reversed(range(n_pole))]


def per_device(sizes, ancestor_inverse, lower_factor, upper_factor, diag_inverse, pole_weights):
    n_pole, n_row, n_col = sizes
    poles, _, rows, cols = ancestor_inverse.shape
    nodes, _, s_row, _ = lower_factor.shape
    size = s_row * n_row
    per_col = size // n_col
    p, r, c = (lax.axis_index(name) for name in ("pole", "row", "col"))

    if n_row == 2:
        halves = 2
        other = lax.ppermute(lower_factor, "row", [(0, 1), (1, 0)])
        s = jnp.stack([lower_factor, other]).reshape(nodes * 2 * size, cols)
    else:
        halves = 1
        s = lax.all_gather(lower_factor, "row", axis=2, tiled=True).reshape(-1, cols)
    s8 = s.astype(LO_FACTOR)
    half = size // halves

    top = jnp.max(jnp.abs(pole_weights)) * poles
    scale = jnp.where(top > 0, 2.0**19 / jnp.maximum(top, 1e-30), 1.0)
    weights = jnp.concatenate([(pole_weights * scale).reshape(-1), (1.0 / scale).reshape(1)])

    weight_real = pole_weights[:, 0].reshape(-1, 1, 1, 1)
    weight_imag = pole_weights[:, 1].reshape(-1, 1, 1, 1)
    weighted_diag = jnp.sum(
        weight_real * diag_inverse[:, :, 1] + weight_imag * diag_inverse[:, :, 0], axis=0
    ).transpose(0, 2, 1)
    weights, weighted_diag = lax.optimization_barrier((weights, weighted_diag))

    quarter = rows // n_pole
    widths, calls = plan_of(rows, n_pole)
    firsts = [sum(widths[:g]) for g in range(len(widths))]
    tile = min(256, *widths)
    step = min(1024, rows)

    numbers, starts = [], []
    for runs in calls:
        starts.append(len(numbers))
        for g, k in runs:
            base = (peer(p, k, n_pole) * quarter + firsts[g]) // tile
            numbers += [base + j for j in range(widths[g] // tile)]
    puts = []
    for first in firsts:
        puts.append(len(numbers))
        numbers += [(back_peer(p, k, n_pole) * quarter + first) // 128 for k in range(n_pole)]
    where = len(numbers)
    for k in range(n_col):
        target = peer(c, k, n_col)
        per_half = half // per_col
        h = target // per_half
        numbers += [h ^ r if halves == 2 else h, target % per_half * per_col]
    owners = len(numbers)
    numbers += [(c + n_col - k) % n_col for k in range(n_col)]
    scalars = jnp.stack([jnp.asarray(x, jnp.int32) for x in numbers])

    mine = lax.dynamic_slice_in_dim(upper_factor[:, 0], p * quarter, quarter, 2)
    upper = [jnp.concatenate([upper_factor[:, 1], mine], axis=2)]
    for _ in range(1, n_col):
        ring = [(i, (i + 1) % n_col) for i in range(n_col)]
        upper.append(lax.ppermute(upper[-1], "col", ring))

    real = out = None
    shared = []
    done = {g: {} for g in range(len(widths))}
    for i, runs in enumerate(calls):
        real, *results = main_call(
            [k > 0 for _, k in runs], [widths[g] for g, _ in runs], halves, nodes, tile,
            scalars, starts[i], weights, ancestor_inverse, s, s8, real,
        )
        for (g, k), result in zip(runs, results, strict=True):
            if k:
                result = send(result, "pole", k, n_pole)
            done[g][k] = result
        for g, got in done.items():
            if got is None or len(got) < n_pole:
                continue
            done[g] = None
            own, received = got[0], [got[k] for k in range(1, n_pole)]
            own, *parts = pole_call(
                halves, nodes, per_col, n_col, tile, scalars, where, own, received
            )
            received = []
            for k, x in enumerate(parts):
                received.append(send(x, "col", k + 1, n_col))
            projected, payload = col_call(
                tile, nodes, scalars, owners, own, received, upper, rows + firsts[g]
            )
            shared.append(projected)
            payloads = [payload]
            for k in range(1, n_pole):
                payloads.append(send(payload, "pole", k, n_pole))
            out = place_call(rows, scalars, puts[g], payloads, out)

    parts = project_call(halves, nodes, per_col, n_col, step, scalars, where, owners, real, upper)
    shared.append(parts[0])
    for k in range(1, n_col):
        shared.append(send(parts[k], "col", k, n_col))
    shared = sum(shared[1:], shared[0])
    if n_row == 2:
        keep = lax.dynamic_slice_in_dim(shared, r * s_row, s_row, 2)
        give = lax.dynamic_slice_in_dim(shared, (1 - r) * s_row, s_row, 2)
        shared = keep + lax.ppermute(give, "row", [(0, 1), (1, 0)])
    else:
        shared = lax.psum_scatter(shared, "row", scatter_dimension=2, tiled=True)
    mine = weighted_diag - shared
    if n_pole & (n_pole - 1) == 0:
        terms = [mine]
        for k in range(1, n_pole):
            terms.append(send(mine, "pole", k, n_pole))
        diag = tree_sum(terms)
    else:
        diag = lax.psum(mine, "pole")
    density = out.reshape(nodes, per_col, rows).transpose(2, 0, 1)
    return density, diag.transpose(0, 2, 1)


def solution(mesh):
    sizes = tuple(mesh.shape[name] for name in ("pole", "row", "col"))
    placed = (
        P("pole", None, "row", "col"),
        P(None, None, "row", "col"),
        P(None, None, "col", "row"),
        P("pole", None, None, "row", "col"),
        P("pole", None),
    )

    def body(ancestor_inverse, *rest):
        return per_device(sizes, ancestor_inverse, *rest)

    return jax.shard_map(
        body,
        mesh=mesh,
        in_specs=placed,
        out_specs=(P("row", None, "col"), P(None, "row", "col")),
        check_vma=False,
    )
```

```python
import functools

import jax
import jax.numpy as jnp
from jax import lax
from jax.experimental import pallas as pl
from jax.experimental.pallas import tpu as pltpu
from jax.sharding import PartitionSpec as P


F32 = jnp.float32
BF16 = jnp.bfloat16
LO = jnp.float8_e4m3fn
LO_FACTOR = jnp.float8_e5m2
SPAN = 250.0
PAD = 16
NT = (((1,), (1,)), ((), ()))


def dot_nt(a, b):
    return lax.dot_general(a, b, NT, preferred_element_type=F32)


def encode(x):
    top = jnp.max(jnp.abs(x), axis=0, keepdims=True)
    scale = (top * 1.01).astype(BF16).astype(F32)
    inverse = jnp.where(scale > 1e-30, SPAN / jnp.maximum(scale, 1e-30), 0.0)
    size = jnp.exp2(jnp.abs(x) * inverse - SPAN / 2)
    code = jnp.where(x < 0, -size, size).astype(BF16)
    return code, jnp.broadcast_to(scale, (PAD, x.shape[1])).astype(BF16)


def decode(payload):
    rows = payload.shape[0] - PAD
    code = payload[:rows].astype(F32)
    scale = payload[rows:].astype(F32)[:1] * (1.0 / SPAN)
    size = (jnp.log2(jnp.abs(code)) + SPAN / 2) * scale
    return jnp.where(code < 0, -size, size)


def write_payload(ref, x):
    rows = x.shape[0]
    code, scale = encode(x)
    ref[:rows] = code
    ref[rows:] = scale


def main_body(outs, steps, halves, nodes, base_ref, w_ref, g_ref, *rest):
    s_ref, s8_ref = rest[:2]
    zr_ref, out_refs = rest[-1 - len(outs)], rest[len(rest) - len(outs) :]
    poles = g_ref.shape[0]
    w_real = w_imag = None
    for p in range(poles):
        a, b = w_ref[2 * p], w_ref[2 * p + 1]
        real, imag = g_ref[p, 0].astype(F32), g_ref[p, 1].astype(F32)
        x, y = a * real - b * imag, a * imag + b * real
        w_real = x if w_real is None else w_real + x
        w_imag = y if w_imag is None else w_imag + y
    hi_real, hi_imag = w_real.astype(BF16), w_imag.astype(BF16)
    lo_real = (w_real - hi_real.astype(F32)).astype(LO)
    lo_imag = (w_imag - hi_imag.astype(F32)).astype(LO)
    back = -w_ref[2 * poles]
    x = dot_nt(s_ref[...], hi_real) + dot_nt(s8_ref[...], lo_real)
    y = dot_nt(s_ref[...], hi_imag) + dot_nt(s8_ref[...], lo_imag)
    half = x.shape[0] // (halves * nodes * 2)
    shape = (halves * nodes, 2, half, x.shape[1])
    x, y = x.reshape(shape), y.reshape(shape)
    flat = (halves * nodes * half, x.shape[3])
    zr_ref[...] = ((x[:, 0] - y[:, 1]) * back).reshape(flat)
    z_imag = ((x[:, 1] + y[:, 0]) * back).reshape(flat)
    if any(outs):
        code, scale = encode(z_imag)
    first = 0
    for remote, count, out_ref in zip(outs, steps, out_refs, strict=True):
        j = pl.program_id(0)

        @pl.when((j >= first) & (j < first + count))
        def _(remote=remote, out_ref=out_ref):
            if remote:
                out_ref[: z_imag.shape[0]] = code
                out_ref[z_imag.shape[0] :] = scale
            else:
                out_ref[...] = z_imag

        first += count


def main_call(outs, widths, halves, nodes, tile, scalars, at, weights, blocks, s, s8, real):
    poles, _, rows, cols = blocks.shape
    flat = s.shape[0] // 2
    steps = [w // tile for w in widths]
    aliased = [] if real is None else [real]
    out_specs, out_shape, first = [], [], 0
    for remote, width, count in zip(outs, widths, steps, strict=True):
        height = flat + PAD if remote else flat
        out_specs.append(
            pl.BlockSpec(
                (height, tile),
                lambda j, b, f=first, n=count: (0, jnp.clip(j - f, 0, n - 1)),
            )
        )
        out_shape.append(jax.ShapeDtypeStruct((height, width), BF16 if remote else F32))
        first += count
    whole = pl.BlockSpec(memory_space=pltpu.VMEM)
    grid_spec = pltpu.PrefetchScalarGridSpec(
        num_scalar_prefetch=1,
        grid=(sum(steps),),
        in_specs=[
            pl.BlockSpec(memory_space=pltpu.SMEM),
            pl.BlockSpec((poles, 2, tile, cols), lambda j, b: (0, 0, b[at + j], 0)),
        ]
        + [whole] * 2
        + [pl.BlockSpec(memory_space=pl.ANY)] * len(aliased),
        out_specs=[pl.BlockSpec((flat, tile), lambda j, b: (0, b[at + j]))] + out_specs,
    )
    return pl.pallas_call(
        functools.partial(main_body, outs, steps, halves, nodes),
        grid_spec=grid_spec,
        out_shape=[jax.ShapeDtypeStruct((flat, rows), F32)] + out_shape,
        input_output_aliases={5: 0} if aliased else {},
        compiler_params=pltpu.CompilerParams(vmem_limit_bytes=32 << 20),
        name="products",
    )(scalars, weights, blocks, s, s8, *aliased)


def pole_body(nodes, per_col, n_in, at, where_ref, own_ref, *rest):
    ins, outs, z_ref = rest[:n_in], rest[n_in:-1], rest[-1]
    z = own_ref[...]
    for ref in ins:
        z = z + decode(ref[...])
    z_ref[...] = z.reshape(z_ref.shape)
    for k, out in enumerate(outs):
        h = where_ref[at + 2 * k]
        first = pl.multiple_of(where_ref[at + 2 * k + 1], per_col)
        part = z_ref[h, :, pl.ds(first, per_col), :]
        part = part.reshape(nodes * per_col, part.shape[2])
        if k:
            write_payload(out, part)
        else:
            out[...] = part


def pole_call(halves, nodes, per_col, n_col, tile, scalars, at, own, received):
    flat, width = own.shape
    block = lambda rows: pl.BlockSpec((rows, tile), lambda j, w: (0, j))
    part = nodes * per_col
    return pl.pallas_call(
        functools.partial(pole_body, nodes, per_col, len(received), at),
        grid_spec=pltpu.PrefetchScalarGridSpec(
            num_scalar_prefetch=1,
            grid=(width // tile,),
            in_specs=[block(flat)] + [block(flat + PAD)] * len(received),
            out_specs=[block(part)] + [block(part + PAD)] * (n_col - 1),
            scratch_shapes=[pltpu.VMEM((halves, nodes, flat // (halves * nodes), tile), F32)],
        ),
        out_shape=[jax.ShapeDtypeStruct((part, width), F32)]
        + [jax.ShapeDtypeStruct((part + PAD, width), BF16)] * (n_col - 1),
        compiler_params=pltpu.CompilerParams(vmem_limit_bytes=16 << 20),
        name="pole_sum",
    )(scalars, own, *received)


def far(x):
    return pltpu.with_memory_space_constraint(x, pltpu.HBM)


def gathered(u_refs, all_ref, owner_ref, at):
    for k, ref in enumerate(u_refs):
        all_ref[owner_ref[at + k]] = ref[...]
    blocks, nodes = all_ref.shape[:2]
    return [jnp.concatenate([all_ref[k, n] for k in range(blocks)], axis=0) for n in range(nodes)]


def col_body(nodes, n_col, at, owner_ref, own_ref, *rest):
    u_refs, ins, (shared_ref, out_ref, all_ref) = rest[:n_col], rest[n_col:-3], rest[-3:]
    u = gathered(u_refs, all_ref, owner_ref, at)
    z = own_ref[...]
    for ref in ins:
        z = z + decode(ref[...])
    write_payload(out_ref, z)
    half = z.shape[0] // nodes
    hi, lo = split(z)

    @pl.when(pl.program_id(0) == 0)
    def _():
        shared_ref[...] = jnp.zeros_like(shared_ref)

    for n in range(nodes):
        rows = slice(n * half, (n + 1) * half)
        shared_ref[n] += dot_nt(hi[rows], u[n]) + dot_nt(lo[rows], u[n])


def col_call(tile, nodes, scalars, at, own, received, u, first, last):
    part, width = own.shape
    block = lambda rows: pl.BlockSpec((rows, tile), lambda j, w: (0, j))
    some = u[0].shape[1]
    shared = jax.ShapeDtypeStruct((nodes, part // nodes, some * len(u)), F32)
    return pl.pallas_call(
        functools.partial(col_body, nodes, len(u), at),
        grid_spec=pltpu.PrefetchScalarGridSpec(
            num_scalar_prefetch=1,
            grid=(width // tile,),
            in_specs=[block(part)]
            + [pl.BlockSpec((nodes, some, tile), lambda j, w: (0, 0, first // tile + j))] * len(u)
            + [block(part + PAD)] * len(received),
            out_specs=[pl.BlockSpec(shared.shape, lambda j, w: (0, 0, 0)), block(part + PAD)],
            scratch_shapes=[pltpu.VMEM((len(u), nodes, some, tile), BF16)],
        ),
        out_shape=[shared, jax.ShapeDtypeStruct((part + PAD, width), BF16)],
        compiler_params=pltpu.CompilerParams(vmem_limit_bytes=16 << 20),
        name="col_sum",
    )(scalars, own, *(far(x) for x in u), *(received if last else [far(x) for x in received]))


def place_body(n_in, at, at_ref, *rest):
    ins, out_ref, z_ref, sems = rest[:n_in], rest[-3], rest[-2], rest[-1]
    width = z_ref.shape[2]
    copies = []
    for k, ref in enumerate(ins):
        z_ref[k] = decode(ref[...])
        first = pl.multiple_of(at_ref[at + k] * 128, 128)
        copy = pltpu.make_async_copy(z_ref.at[k], out_ref.at[:, pl.ds(first, width)], sems.at[k])
        copy.start()
        copies.append(copy)
    for copy in copies:
        copy.wait()


def place_call(rows, scalars, at, payloads, out):
    part, width = payloads[0].shape[0] - PAD, payloads[0].shape[1]
    n = len(payloads)
    aliased = [] if out is None else [out]
    return pl.pallas_call(
        functools.partial(place_body, n, at),
        in_specs=[pl.BlockSpec(memory_space=pltpu.SMEM)]
        + [pl.BlockSpec(memory_space=pltpu.VMEM)] * n
        + [pl.BlockSpec(memory_space=pl.ANY)] * len(aliased),
        out_specs=pl.BlockSpec(memory_space=pl.ANY),
        out_shape=jax.ShapeDtypeStruct((part, rows), F32),
        scratch_shapes=[pltpu.VMEM((n, part, width), F32), pltpu.SemaphoreType.DMA((n,))],
        input_output_aliases={1 + n: 0} if aliased else {},
        compiler_params=pltpu.CompilerParams(vmem_limit_bytes=16 << 20),
        name="place",
    )(scalars, *payloads, *aliased)


def split(x):
    hi = x.astype(BF16)
    return hi, (x - hi.astype(F32)).astype(BF16)


def project_body(halves, nodes, per_col, n_col, at, owners, where_ref, z_ref, *rest):
    u_refs, outs, (acc_ref, all_ref) = rest[:n_col], rest[n_col:-2], rest[-2:]
    u = gathered(u_refs, all_ref, where_ref, owners)
    half = z_ref.shape[0] // (halves * nodes)
    step = pl.program_id(0)

    @pl.when(step == 0)
    def _():
        acc_ref[...] = jnp.zeros_like(acc_ref)

    for n in range(nodes):
        rows = [split(z_ref[pl.ds((h * nodes + n) * half, half)]) for h in range(halves)]
        both = jnp.concatenate([x[0] for x in rows] + [x[1] for x in rows], axis=0)
        result = dot_nt(both, u[n])
        for h in range(halves):
            low = result[(halves + h) * half : (halves + h + 1) * half]
            acc_ref[h, n] += result[h * half : (h + 1) * half] + low

    @pl.when(step == pl.num_programs(0) - 1)
    def _():
        for k, out in enumerate(outs):
            first = pl.multiple_of(where_ref[at + 2 * k + 1], per_col)
            out[...] = acc_ref[where_ref[at + 2 * k], :, pl.ds(first, per_col), :]


def project_call(halves, nodes, per_col, n_col, tile, scalars, at, owners, z, u):
    flat, rows = z.shape
    some = u[0].shape[1]
    size = some * n_col
    out = jax.ShapeDtypeStruct((nodes, per_col, size), F32)
    return pl.pallas_call(
        functools.partial(project_body, halves, nodes, per_col, n_col, at, owners),
        grid_spec=pltpu.PrefetchScalarGridSpec(
            num_scalar_prefetch=1,
            grid=(rows // tile,),
            in_specs=[
                pl.BlockSpec((flat, tile), lambda j, w: (0, j)),
            ]
            + [pl.BlockSpec((nodes, some, tile), lambda j, w: (0, 0, j))] * n_col,
            out_specs=[pl.BlockSpec(out.shape, lambda j, w: (0, 0, 0))] * n_col,
            scratch_shapes=[
                pltpu.VMEM((halves, nodes, flat // (halves * nodes), size), F32),
                pltpu.VMEM((n_col, nodes, some, tile), BF16),
            ],
        ),
        out_shape=[out] * n_col,
        compiler_params=pltpu.CompilerParams(vmem_limit_bytes=24 << 20),
        name="project",
    )(scalars, z, *u)


def peer(i, k, n):
    return i ^ k if n & (n - 1) == 0 else (i + k) % n


def back_peer(i, k, n):
    return i ^ k if n & (n - 1) == 0 else (i + n - k) % n


def send(x, axis, k, n):
    return lax.ppermute(x, axis, [(i, peer(i, k, n)) for i in range(n)])


def tree_sum(parts):
    while len(parts) > 1:
        parts = [a + b for a, b in zip(parts[::2], parts[1::2], strict=True)]
    return parts[0]


def plan_of(rows, n_pole):
    quarter = rows // n_pole
    if quarter % 1024 == 0 and n_pole == 4:
        widths = [quarter * 3 // 4, quarter // 4]
        calls = [[(0, 3), (0, 2)], [(0, 1), (0, 0)], [(1, 3), (1, 2), (1, 1)], [(1, 0)]]
        return widths, calls
    return [quarter], [[(0, k)] for k in reversed(range(n_pole))]


def per_device(sizes, ancestor_inverse, lower_factor, upper_factor, diag_inverse, pole_weights):
    n_pole, n_row, n_col = sizes
    poles, _, rows, cols = ancestor_inverse.shape
    nodes, _, s_row, _ = lower_factor.shape
    size = s_row * n_row
    per_col = size // n_col
    p, r, c = (lax.axis_index(name) for name in ("pole", "row", "col"))

    if n_row == 2:
        halves = 2
        other = lax.ppermute(lower_factor, "row", [(0, 1), (1, 0)])
        s = jnp.stack([lower_factor, other]).reshape(nodes * 2 * size, cols)
    else:
        halves = 1
        s = lax.all_gather(lower_factor, "row", axis=2, tiled=True).reshape(-1, cols)
    s8 = s.astype(LO_FACTOR)
    half = size // halves

    top = jnp.max(jnp.abs(pole_weights)) * poles
    scale = jnp.where(top > 0, 2.0**19 / jnp.maximum(top, 1e-30), 1.0)
    weights = jnp.concatenate([(pole_weights * scale).reshape(-1), (1.0 / scale).reshape(1)])

    weight_real = pole_weights[:, 0].reshape(-1, 1, 1, 1)
    weight_imag = pole_weights[:, 1].reshape(-1, 1, 1, 1)
    weighted_diag = jnp.sum(
        weight_real * diag_inverse[:, :, 1] + weight_imag * diag_inverse[:, :, 0], axis=0
    ).transpose(0, 2, 1)
    weights, weighted_diag = lax.optimization_barrier((weights, weighted_diag))

    quarter = rows // n_pole
    widths, calls = plan_of(rows, n_pole)
    firsts = [sum(widths[:g]) for g in range(len(widths))]
    tile = min(256, *widths)
    step = min(1024, rows)

    numbers, starts = [], []
    for runs in calls:
        starts.append(len(numbers))
        for g, k in runs:
            base = (peer(p, k, n_pole) * quarter + firsts[g]) // tile
            numbers += [base + j for j in range(widths[g] // tile)]
    puts = []
    for first in firsts:
        puts.append(len(numbers))
        numbers += [(back_peer(p, k, n_pole) * quarter + first) // 128 for k in range(n_pole)]
    where = len(numbers)
    for k in range(n_col):
        target = peer(c, k, n_col)
        per_half = half // per_col
        h = target // per_half
        numbers += [h ^ r if halves == 2 else h, target % per_half * per_col]
    owners = len(numbers)
    numbers += [(c + n_col - k) % n_col for k in range(n_col)]
    scalars = jnp.stack([jnp.asarray(x, jnp.int32) for x in numbers])

    mine = lax.dynamic_slice_in_dim(upper_factor[:, 0], p * quarter, quarter, 2)
    upper = [jnp.concatenate([upper_factor[:, 1], mine], axis=2)]
    for _ in range(1, n_col):
        ring = [(i, (i + 1) % n_col) for i in range(n_col)]
        upper.append(lax.ppermute(upper[-1], "col", ring))

    real = out = None
    shared = []
    done = {g: {} for g in range(len(widths))}
    for i, runs in enumerate(calls):
        real, *results = main_call(
            [k > 0 for _, k in runs], [widths[g] for g, _ in runs], halves, nodes, tile,
            scalars, starts[i], weights, ancestor_inverse, s, s8, real,
        )
        for (g, k), result in zip(runs, results, strict=True):
            if k:
                result = send(result, "pole", k, n_pole)
            done[g][k] = result
        for g, got in done.items():
            if got is None or len(got) < n_pole:
                continue
            done[g] = None
            own, received = got[0], [got[k] for k in range(1, n_pole)]
            own, *parts = pole_call(
                halves, nodes, per_col, n_col, tile, scalars, where, own, received
            )
            received = []
            for k, x in enumerate(parts):
                received.append(send(x, "col", k + 1, n_col))
            projected, payload = col_call(
                tile, nodes, scalars, owners, own, received, upper, rows + firsts[g],
                g == len(widths) - 1,
            )
            shared.append(projected)
            payloads = [payload]
            for k in range(1, n_pole):
                payloads.append(send(payload, "pole", k, n_pole))
            out = place_call(rows, scalars, puts[g], payloads, out)

    parts = project_call(halves, nodes, per_col, n_col, step, scalars, where, owners, real, upper)
    shared.append(parts[0])
    for k in range(1, n_col):
        shared.append(send(parts[k], "col", k, n_col))
    shared = sum(shared[1:], shared[0])
    if n_row == 2:
        keep = lax.dynamic_slice_in_dim(shared, r * s_row, s_row, 2)
        give = lax.dynamic_slice_in_dim(shared, (1 - r) * s_row, s_row, 2)
        shared = keep + lax.ppermute(give, "row", [(0, 1), (1, 0)])
    else:
        shared = lax.psum_scatter(shared, "row", scatter_dimension=2, tiled=True)
    mine = weighted_diag - shared
    if n_pole & (n_pole - 1) == 0:
        terms = [mine]
        for k in range(1, n_pole):
            terms.append(send(mine, "pole", k, n_pole))
        diag = tree_sum(terms)
    else:
        diag = lax.psum(mine, "pole")
    density = out.reshape(nodes, per_col, rows).transpose(2, 0, 1)
    return density, diag.transpose(0, 2, 1)


def solution(mesh):
    sizes = tuple(mesh.shape[name] for name in ("pole", "row", "col"))
    placed = (
        P("pole", None, "row", "col"),
        P(None, None, "row", "col"),
        P(None, None, "col", "row"),
        P("pole", None, None, "row", "col"),
        P("pole", None),
    )

    def body(ancestor_inverse, *rest):
        return per_device(sizes, ancestor_inverse, *rest)

    return jax.shard_map(
        body,
        mesh=mesh,
        in_specs=placed,
        out_specs=(P("row", None, "col"), P(None, "row", "col")),
        check_vma=False,
    )
```
